32 devices in a mesh: group: 4 (over x, core), member: 8 (over z, y).
Axes of the slice: x: 2, y: 2, z: 4, core: 2. Of those that a mesh axis runs over, the one named last changes fastest.
Arguments:
- activations: bfloat16 [8192, 1152], P(('group', 'member')), may hold values from -6 to 6
- routes: int32 [8192, 1], P(('group', 'member')), may hold values from 0 to 31; in each aligned block of 256 rows (0 to 255, 256 to 511, ...) at most 16 rows name the same one
- centre_bias: float32 [1152], replicated, may hold values from -2 to 2
- centre_first: float32 [1152], replicated, may hold values from -600 to 600
- centre_second: float32 [1152], replicated, may hold values from 1000 to 1000000
- router: bfloat16 [32, 1152], P(('group', 'member')), may hold values from -0.1875 to 0.1875
- router_first: float32 [32, 1152], P(('group', 'member')), may hold values from -180 to 180
- router_second: float32 [32, 1152], P(('group', 'member')), may hold values from 100 to 100000
- encoder: bfloat16 [32, 1152, 512], P(('group', 'member')), may hold values from -0.1875 to 0.1875
- enc_bias: float32 [32, 512], P(('group', 'member')), may hold values from -3 to 3
- decoder: bfloat16 [32, 512, 1152], P(('group', 'member')), may hold values from -0.25 to 0.25
- encoder_first: float32 [32, 1152, 512], P(('group', 'member')), may hold values from -30 to 30
- encoder_second: float32 [32, 1152, 512], P(('group', 'member')), may hold values from 1 to 1000
- enc_bias_first: float32 [32, 512], P(('group', 'member')), may hold values from -60 to 60
- enc_bias_second: float32 [32, 512], P(('group', 'member')), may hold values from 10 to 10000
- decoder_first: float32 [32, 512, 1152], P(('group', 'member')), may hold values from -30 to 30
- decoder_second: float32 [32, 512, 1152], P(('group', 'member')), may hold values from 1 to 1000
Outputs:
- recon: bfloat16 [8192, 1152], P(('group', 'member'))
- new_centre: float32 [1152], replicated
- new_centre_first: float32 [1152], replicated
- new_centre_second: float32 [1152], replicated
- new_router: bfloat16 [32, 1152], P(('group', 'member'))
- new_router_first: float32 [32, 1152], P(('group', 'member'))
- new_router_second: float32 [32, 1152], P(('group', 'member'))
- new_encoder: bfloat16 [32, 1152, 512], P(('group', 'member'))
- new_enc_bias: float32 [32, 512], P(('group', 'member'))
- new_decoder: bfloat16 [32, 512, 1152], P(('group', 'member'))
- new_encoder_first: float32 [32, 1152, 512], P(('group', 'member'))
- new_encoder_second: float32 [32, 1152, 512], P(('group', 'member'))
- new_enc_bias_first: float32 [32, 512], P(('group', 'member'))
- new_enc_bias_second: float32 [32, 512], P(('group', 'member'))
- new_decoder_first: float32 [32, 512, 1152], P(('group', 'member'))
- new_decoder_second: float32 [32, 512, 1152], P(('group', 'member'))
The draws below stay inside these ranges and needn't reach their ends.
Inputs may be any that keep to these rules, and one draw needn't show every extreme that they name: `routes`: each row names the one expert that serves it. At most 16 rows of one device name the same expert, and in every draw some device's rows name some expert exactly 16 times.
All inputs are finite; a program needn't handle non-finite values.
Results may differ from the reference program's by a relative error of at most 0.009.
Values may be sent and summed in bfloat16 or wider, within the bound.
A program may use at most 128 MiB of HBM per device.

```python
import math
import jax
import jax.numpy as jnp
import numpy as np
from jax import lax

D = 1152
LATENTS = 512
STEP = 10
TOK_DEV = 256
EXPERTS = 32
CAP = 16
TOKENS = 8192
N_GROUP = 4
N_MEMBER = 8


def block_scale(own_key, shape, cuts, least, high):
    level = 1.0
    for dim, parts in cuts:
        heights = jax.random.uniform(jax.random.fold_in(jax.random.fold_in(own_key, 6), dim), (parts,), jnp.float32, least / len(cuts), high / len(cuts))
        level = level * jnp.repeat(jnp.exp(heights), shape[dim] // parts).reshape((-1,) + (1,) * (len(shape) - 1 - dim))
    return level


def deal_out(own_key, own, number, rows, amount, top, limit, lean):
    sequence = jax.random.permutation(own_key, amount)
    packed, common = shares(amount, rows * top, limit, lean, True), shares(amount, rows * top, limit, lean, False)
    places = jnp.arange(amount)

    def named(lengths, rotation):
        used = int((lengths > 0).sum())
        fixed = max(1, used // 4)
        moved = fixed + (places - fixed + rotation * (used - fixed)) % max(1, amount - fixed)
        return jnp.zeros((amount,), jnp.int32).at[sequence[jnp.where(places < fixed, places, moved)]].set(jnp.asarray(lengths, jnp.int32))

    lengths = jnp.where(number % 4 == 0, named(packed, number // 4), named(common, number - number // 4 - 1))
    mixed = jax.random.permutation(jax.random.fold_in(own, 3), amount)
    source_of, receiver = mixed[0:amount // 2 * 2:2], mixed[1:amount // 2 * 2:2]
    margin = jnp.minimum(lengths[source_of] - 1, limit - lengths[receiver]) // 2
    margin = jnp.where((source_of == sequence[0]) | (receiver == sequence[0]) | (lengths[receiver] == 0), 0, jnp.maximum(margin, 0))
    moved = jax.random.randint(jax.random.fold_in(own, 4), (amount // 2,), 0, 1 << 20) % (margin + 1)
    lengths = lengths.at[source_of].add(-moved).at[receiver].add(moved)
    items = jnp.searchsorted(jnp.cumsum(lengths), jnp.arange(rows * top), side="right").astype(jnp.int32)
    grid = items.reshape(top, rows).T
    grid = grid[jax.random.permutation(jax.random.fold_in(own, 1), rows)]
    rotation = jax.random.randint(jax.random.fold_in(own, 2), (rows, 1), 0, top)
    return jnp.take_along_axis(grid, (jnp.arange(top)[None, :] + rotation) % top, axis=1)


def shares(number_of, total, bound, slope, full):
    weights = [(1 << 20) // math.isqrt(standing ** slope) + 1 for standing in range(1, number_of + 1)]
    largest = bound if full else min(bound, max(-(-total // number_of), total * weights[0] // sum(weights)))
    least = 1 if total - largest >= number_of - 1 else 0
    given, rest = [largest] + [least] * (number_of - 1), total - largest - least * (number_of - 1)
    while rest > 0:
        candidates = [i for i in range(1, number_of) if given[i] < largest] or [i for i in range(1, number_of) if given[i] < bound]
        whole, left = sum([weights[i] for i in candidates]), rest
        for i in candidates:
            more = min(bound - given[i], max(1, left * weights[i] // whole), rest)
            given[i] = given[i] + more
            rest = rest - more
    return np.array(given)


def scatter_about(key, extent, scale, limit, shards=(), held_as=jnp.bfloat16):
    factor_of = block_scale(key, extent, shards, -0.22, 0.18) if shards else 1.0
    array = jax.random.normal(key, extent, jnp.float32) * scale * factor_of
    return jnp.minimum(jnp.maximum(array, -limit), limit).astype(held_as)


def setup_inputs(seed: int = 0) -> dict:
    key_of = jax.random.split(jax.random.key(seed), 18)
    activations = scatter_about(key_of[0], (TOKENS, D), 1.0, 6.0, ((0, 32),))
    routes_keys = jax.random.split(jax.random.fold_in(key_of[1], 1), TOKENS // TOK_DEV)
    routes_turns = jax.random.permutation(jax.random.fold_in(key_of[1], 3), TOKENS // TOK_DEV)
    routes = jax.vmap(lambda own, number: deal_out(jax.random.fold_in(key_of[1], 2), own, number, TOK_DEV, EXPERTS, 1, CAP, 2))(routes_keys, routes_turns).reshape((TOKENS, 1))
    centre_bias = scatter_about(key_of[2], (D,), 0.3, 2.0, (), jnp.float32)
    centre_first = scatter_about(key_of[3], (D,), 100.0, 600.0, (), jnp.float32)
    centre_second = jnp.clip(jnp.exp(jax.random.uniform(key_of[4], (D,), jnp.float32, math.log(1000.0), math.log(1000000))), 1000.0, 1000000)
    router = scatter_about(key_of[5], (EXPERTS, D), D ** -0.5, 0.1875, ((0, 32),))
    router_first = scatter_about(key_of[6], (EXPERTS, D), 30.0, 180.0, ((0, 32),), jnp.float32)
    router_second = jnp.clip(jnp.exp(math.log(100000.0) - 6.9077553 * jax.random.uniform(key_of[7], (EXPERTS, D), jnp.float32) ** block_scale(key_of[7], (EXPERTS, D), ((0, 32),), -0.2, 0.2)), 100.0, 100000.0)
    encoder = scatter_about(key_of[8], (EXPERTS, D, LATENTS), D ** -0.5, 0.1875, ((0, 32),))
    enc_bias = scatter_about(key_of[9], (EXPERTS, LATENTS), 0.5, 3.0, ((0, 32),), jnp.float32)
    decoder = scatter_about(key_of[10], (EXPERTS, LATENTS, D), LATENTS ** -0.5, 0.25, ((0, 32),))
    encoder_first = scatter_about(key_of[11], (EXPERTS, D, LATENTS), 5.0, 30.0, ((0, 32),), jnp.float32)
    encoder_second = jnp.clip(jnp.exp(math.log(1000.0) - 6.9077553 * jax.random.uniform(key_of[12], (EXPERTS, D, LATENTS), jnp.float32) ** block_scale(key_of[12], (EXPERTS, D, LATENTS), ((0, 32),), -0.2, 0.2)), 1.0, 1000.0)
    enc_bias_first = scatter_about(key_of[13], (EXPERTS, LATENTS), 10.0, 60.0, ((0, 32),), jnp.float32)
    enc_bias_second = jnp.clip(jnp.exp(math.log(10000.0) - 6.9077553 * jax.random.uniform(key_of[14], (EXPERTS, LATENTS), jnp.float32) ** block_scale(key_of[14], (EXPERTS, LATENTS), ((0, 32),), -0.2, 0.2)), 10.0, 10000.0)
    decoder_first = scatter_about(key_of[15], (EXPERTS, LATENTS, D), 5.0, 30.0, ((0, 32),), jnp.float32)
    decoder_second = jnp.clip(jnp.exp(math.log(1000.0) - 6.9077553 * jax.random.uniform(key_of[16], (EXPERTS, LATENTS, D), jnp.float32) ** block_scale(key_of[16], (EXPERTS, LATENTS, D), ((0, 32),), -0.2, 0.2)), 1.0, 1000.0)
    return {"activations": activations, "routes": routes, "centre_bias": centre_bias, "centre_first": centre_first, "centre_second": centre_second, "router": router, "router_first": router_first, "router_second": router_second, "encoder": encoder, "enc_bias": enc_bias, "decoder": decoder, "encoder_first": encoder_first, "encoder_second": encoder_second, "enc_bias_first": enc_bias_first, "enc_bias_second": enc_bias_second, "decoder_first": decoder_first, "decoder_second": decoder_second}


learn_rate = 0.001
beta_one = 0.9
beta_two = 0.999
adam_eps = 1e-08
sparsity = 0.1

def adam_update(weights_in, gradient, moment_one, moment_two):
    first_new = beta_one * moment_one + (1.0 - beta_one) * gradient
    second_new = beta_two * moment_two + (1.0 - beta_two) * gradient * gradient
    first_hat = first_new / (1.0 - beta_one ** STEP)
    second_hat = second_new / (1.0 - beta_two ** STEP)
    stepped = weights_in.astype(jnp.float32) - learn_rate * first_hat / (jnp.sqrt(second_hat) + adam_eps)
    return (stepped.astype(weights_in.dtype), first_new, second_new)

def expert_pass(in_rows, live_mask, centre_bias, router_row, encoder, enc_bias, decoder):
    wide_rows = in_rows.astype(jnp.float32)
    centred = (wide_rows - centre_bias).astype(jnp.bfloat16)
    preact = jnp.dot(centred, encoder, preferred_element_type=jnp.float32) + enc_bias
    positive = jnp.maximum(preact, 0.0)
    latents = (positive * positive).astype(jnp.bfloat16)
    logits = jnp.dot(in_rows, router_row, preferred_element_type=jnp.float32)
    gating = jax.nn.sigmoid(logits)
    ungated = jnp.dot(latents, decoder, preferred_element_type=jnp.float32)
    rebuilt = centre_bias + gating[:, None] * ungated
    errors = (wide_rows - rebuilt) * live_mask[:, None]
    backward = (-gating[:, None] * errors).astype(jnp.bfloat16)
    decoder_grad = jnp.dot(latents.T, backward, preferred_element_type=jnp.float32)
    latent_grad = jnp.dot(backward, decoder.T, preferred_element_type=jnp.float32) + sparsity
    preact_grad = (latent_grad * 2.0 * positive * live_mask[:, None]).astype(jnp.bfloat16)
    encoder_grad = jnp.dot(centred.T, preact_grad, preferred_element_type=jnp.float32)
    bias_grad = lax.optimization_barrier(jnp.sum(preact_grad.astype(jnp.float32), axis=0))
    logit_grad = (-lax.optimization_barrier(jnp.sum(errors * ungated, axis=1)) * gating * (1.0 - gating)).astype(jnp.bfloat16)
    router_grad = jnp.dot(logit_grad, in_rows, preferred_element_type=jnp.float32)
    centre_part = -lax.optimization_barrier(jnp.sum(errors, axis=0)) - jnp.dot(encoder.astype(jnp.float32), bias_grad, precision=lax.Precision.HIGHEST)
    return (rebuilt.astype(jnp.bfloat16), (encoder_grad, bias_grad, decoder_grad, router_grad), centre_part)

def reference(activations, routes, centre_bias, centre_first, centre_second, router, router_first, router_second, encoder, enc_bias, decoder, encoder_first, encoder_second, enc_bias_first, enc_bias_second, decoder_first, decoder_second):
    experts = N_GROUP * N_MEMBER
    max_rows = experts * CAP
    tokens = activations.shape[0]
    route_ids = routes[:, 0]

    def per_expert(state_pair, expert_in):
        recon_all, centre_sum = state_pair
        expert_id, router_row, expert_encoder, expert_bias, expert_decoder, moments_in = expert_in
        is_mine = route_ids == expert_id
        row_index = jnp.nonzero(is_mine, size=max_rows, fill_value=0)[0].astype(jnp.int32)
        live_count = jnp.sum(is_mine.astype(jnp.int32))
        live_mask = (jnp.arange(max_rows).astype(jnp.int32) < live_count).astype(jnp.float32)
        in_rows = activations[row_index]
        rebuilt, grads, centre_part = expert_pass(in_rows, live_mask, centre_bias, router_row, expert_encoder, expert_bias, expert_decoder)
        target = jnp.where(live_mask > 0, row_index, tokens).astype(jnp.int32)
        recon_all = recon_all.at[target].set(rebuilt, mode='drop')
        router_new = adam_update(router_row, grads[3], moments_in[0], moments_in[1])
        encoder_new = adam_update(expert_encoder, grads[0], moments_in[2], moments_in[3])
        bias_new = adam_update(expert_bias, grads[1], moments_in[4], moments_in[5])
        decoder_new = adam_update(expert_decoder, grads[2], moments_in[6], moments_in[7])
        return ((recon_all, centre_sum + centre_part), (router_new, encoder_new, bias_new, decoder_new))
    zero_recon = jnp.zeros((tokens, activations.shape[1]), jnp.bfloat16)
    zero_centre = jnp.zeros((activations.shape[1],), jnp.float32)
    expert_ids = jnp.arange(experts).astype(jnp.int32)
    moments_all = (router_first, router_second, encoder_first, encoder_second, enc_bias_first, enc_bias_second, decoder_first, decoder_second)
    (recon_all, centre_grad), stacked = lax.scan(per_expert, (zero_recon, zero_centre), (expert_ids, router, encoder, enc_bias, decoder, moments_all))
    router_new, encoder_new, bias_new, decoder_new = stacked
    centre_new = adam_update(centre_bias, centre_grad, centre_first, centre_second)
    return (recon_all, centre_new[0], centre_new[1], centre_new[2], router_new[0], router_new[1], router_new[2], encoder_new[0], bias_new[0], decoder_new[0], encoder_new[1], encoder_new[2], bias_new[1], bias_new[2], decoder_new[1], decoder_new[2])
```

```python
import jax
import jax.numpy as jnp
from jax import lax
from jax.sharding import PartitionSpec as P

STEP = 10


learn_rate = 0.001
beta_one = 0.9
beta_two = 0.999
adam_eps = 1e-08
sparsity = 0.1
EMPTY = 16.0


def adam_update(weights_in, gradient, moment_one, moment_two):
    first_new = beta_one * moment_one + (1.0 - beta_one) * gradient
    second_new = beta_two * moment_two + (1.0 - beta_two) * gradient * gradient
    first_hat = first_new / (1.0 - beta_one**STEP)
    second_hat = second_new / (1.0 - beta_two**STEP)
    stepped = weights_in.astype(jnp.float32) - learn_rate * first_hat / (
        jnp.sqrt(second_hat) + adam_eps
    )
    return (stepped.astype(weights_in.dtype), first_new, second_new)


def forward_pass(in_rows, centre_bias, router_row, encoder, enc_bias, decoder):
    centred = (in_rows.astype(jnp.float32) - centre_bias).astype(jnp.bfloat16)
    preact = jnp.dot(centred, encoder, preferred_element_type=jnp.float32) + enc_bias
    positive = jnp.maximum(preact, 0.0)
    latents = (positive * positive).astype(jnp.bfloat16)
    router_wide = jnp.broadcast_to(router_row[:, None], (router_row.shape[0], 128))
    logits = jnp.dot(in_rows, router_wide, preferred_element_type=jnp.float32)[:, 0]
    gating = jax.nn.sigmoid(logits)
    ungated = jnp.dot(latents, decoder, preferred_element_type=jnp.float32)
    rebuilt = centre_bias + gating[:, None] * ungated
    return (centred, positive, latents, gating, ungated, rebuilt)


def backward_pass(
    in_rows, live_mask, centred, positive, latents, gating, ungated, rebuilt, encoder, decoder
):
    errors = (in_rows.astype(jnp.float32) - rebuilt) * live_mask[:, None]
    backward = (-gating[:, None] * errors).astype(jnp.bfloat16)
    decoder_grad = jnp.dot(latents.T, backward, preferred_element_type=jnp.float32)
    latent_grad = jnp.dot(backward, decoder.T, preferred_element_type=jnp.float32) + sparsity
    preact_grad = (latent_grad * 2.0 * positive * live_mask[:, None]).astype(jnp.bfloat16)
    encoder_grad = jnp.dot(centred.T, preact_grad, preferred_element_type=jnp.float32)
    bias_grad = jnp.sum(preact_grad.astype(jnp.float32), axis=0)
    logit_grad = (-jnp.sum(errors * ungated, axis=1) * gating * (1.0 - gating)).astype(jnp.bfloat16)
    router_grad = jnp.dot(logit_grad, in_rows, preferred_element_type=jnp.float32)
    centre_part = -jnp.sum(errors, axis=0) - jnp.dot(
        encoder.astype(jnp.float32), bias_grad, precision=lax.Precision.HIGHEST
    )
    return (encoder_grad, bias_grad, decoder_grad, router_grad, centre_part)


def per_device(
    activations,
    routes,
    centre_bias,
    centre_first,
    centre_second,
    router,
    router_first,
    router_second,
    encoder,
    enc_bias,
    decoder,
    encoder_first,
    encoder_second,
    enc_bias_first,
    enc_bias_second,
    decoder_first,
    decoder_second,
):
    groups = lax.axis_size("group")
    members = lax.axis_size("member")
    devices = groups * members
    row_count = activations.shape[0]
    feature_count = activations.shape[1]
    slot_cap = 2 * row_count // devices
    route_ids = routes[:, 0]
    onehot = (route_ids[:, None] == jnp.arange(devices, dtype=jnp.int32)[None, :]).astype(
        jnp.bfloat16
    )
    earlier = (jnp.arange(row_count)[:, None] > jnp.arange(row_count)[None, :]).astype(jnp.bfloat16)
    before = jnp.dot(earlier, onehot, preferred_element_type=jnp.float32)
    slot_rank = jnp.sum(before * onehot.astype(jnp.float32), axis=1).astype(jnp.int32)
    position = route_ids * slot_cap + slot_rank
    chosen = jnp.arange(devices * slot_cap, dtype=jnp.int32)[:, None] == position[None, :]
    select = chosen.astype(jnp.bfloat16)
    used = jnp.any(chosen, axis=1)
    packed = jnp.where(
        used[:, None],
        jnp.dot(select, activations, preferred_element_type=jnp.float32),
        EMPTY,
    ).astype(jnp.bfloat16)
    arrived = lax.all_to_all(
        packed.reshape(devices, slot_cap, feature_count),
        ("group", "member"),
        split_axis=0,
        concat_axis=0,
        tiled=True,
    )
    in_rows = arrived.reshape(devices * slot_cap, feature_count)
    live_mask = (in_rows[:, 0] < 0.5 * EMPTY).astype(jnp.float32)
    centred, positive, latents, gating, ungated, rebuilt = forward_pass(
        in_rows, centre_bias, router[0], encoder[0], enc_bias[0], decoder[0]
    )
    outgoing = rebuilt.astype(jnp.bfloat16)
    returned = lax.all_to_all(
        outgoing.reshape(devices, slot_cap, feature_count),
        ("group", "member"),
        split_axis=0,
        concat_axis=0,
        tiled=True,
    )
    recon = lax.dot_general(
        select,
        returned.reshape(devices * slot_cap, feature_count),
        (((0,), (0,)), ((), ())),
        preferred_element_type=jnp.float32,
    ).astype(jnp.bfloat16)
    encoder_grad, bias_grad, decoder_grad, router_grad, centre_part = backward_pass(
        in_rows,
        live_mask,
        centred,
        positive,
        latents,
        gating,
        ungated,
        rebuilt,
        encoder[0],
        decoder[0],
    )
    router_new = adam_update(router[0], router_grad, router_first[0], router_second[0])
    encoder_new = adam_update(encoder[0], encoder_grad, encoder_first[0], encoder_second[0])
    bias_new = adam_update(enc_bias[0], bias_grad, enc_bias_first[0], enc_bias_second[0])
    decoder_new = adam_update(decoder[0], decoder_grad, decoder_first[0], decoder_second[0])
    centre_all = lax.all_to_all(
        jnp.broadcast_to(centre_part[None], (devices, feature_count)),
        ("group", "member"),
        split_axis=0,
        concat_axis=0,
        tiled=True,
    )
    centre_total = jnp.sum(centre_all, axis=0)
    centre_new = adam_update(centre_bias, centre_total, centre_first, centre_second)
    return (
        recon,
        centre_new[0],
        centre_new[1],
        centre_new[2],
        router_new[0][None],
        router_new[1][None],
        router_new[2][None],
        encoder_new[0][None],
        bias_new[0][None],
        decoder_new[0][None],
        encoder_new[1][None],
        encoder_new[2][None],
        bias_new[1][None],
        bias_new[2][None],
        decoder_new[1][None],
        decoder_new[2][None],
    )


def solution(mesh):
    placed = (
        P(("group", "member"), None),
        P(("group", "member"), None),
        P(),
        P(),
        P(),
        P(("group", "member"), None),
        P(("group", "member"), None),
        P(("group", "member"), None),
        P(("group", "member"), None, None),
        P(("group", "member"), None),
        P(("group", "member"), None, None),
        P(("group", "member"), None, None),
        P(("group", "member"), None, None),
        P(("group", "member"), None),
        P(("group", "member"), None),
        P(("group", "member"), None, None),
        P(("group", "member"), None, None),
    )
    return jax.shard_map(
        per_device,
        mesh=mesh,
        in_specs=placed,
        out_specs=(
            P(("group", "member"), None),
            P(),
            P(),
            P(),
            P(("group", "member"), None),
            P(("group", "member"), None),
            P(("group", "member"), None),
            P(("group", "member"), None, None),
            P(("group", "member"), None),
            P(("group", "member"), None, None),
            P(("group", "member"), None, None),
            P(("group", "member"), None, None),
            P(("group", "member"), None),
            P(("group", "member"), None),
            P(("group", "member"), None, None),
            P(("group", "member"), None, None),
        ),
        check_vma=False,
    )
```

```python
import functools

import jax
import jax.numpy as jnp
from jax import lax
from jax.experimental import pallas as pl
from jax.experimental.pallas import tpu as pltpu
from jax.sharding import PartitionSpec as P

MESH = pl.DeviceIdType.MESH

STEP = 10


learn_rate = 0.001
beta_one = 0.9
beta_two = 0.999
adam_eps = 1e-08
sparsity = 0.1
EMPTY = 16.0


def adam_update(weights_in, gradient, moment_one, moment_two):
    first_new = beta_one * moment_one + (1.0 - beta_one) * gradient
    second_new = beta_two * moment_two + (1.0 - beta_two) * gradient * gradient
    first_hat = first_new / (1.0 - beta_one**STEP)
    second_hat = second_new / (1.0 - beta_two**STEP)
    stepped = weights_in.astype(jnp.float32) - learn_rate * first_hat / (
        jnp.sqrt(second_hat) + adam_eps
    )
    return (stepped.astype(weights_in.dtype), first_new, second_new)


def forward_pass(in_rows, centre_bias, router_row, encoder, enc_bias, decoder):
    centred = (in_rows.astype(jnp.float32) - centre_bias).astype(jnp.bfloat16)
    preact = jnp.dot(centred, encoder, preferred_element_type=jnp.float32) + enc_bias
    positive = jnp.maximum(preact, 0.0)
    latents = (positive * positive).astype(jnp.bfloat16)
    router_wide = jnp.broadcast_to(router_row[:, None], (router_row.shape[0], 128))
    logits = jnp.dot(in_rows, router_wide, preferred_element_type=jnp.float32)[:, 0]
    gating = jax.nn.sigmoid(logits)
    ungated = jnp.dot(latents, decoder, preferred_element_type=jnp.float32)
    rebuilt = centre_bias + gating[:, None] * ungated
    return (centred, positive, latents, gating, ungated, rebuilt)


def backward_pass(
    in_rows, live_mask, centred, positive, latents, gating, ungated, rebuilt, encoder, decoder
):
    errors = (in_rows.astype(jnp.float32) - rebuilt) * live_mask[:, None]
    backward = (-gating[:, None] * errors).astype(jnp.bfloat16)
    decoder_grad = jnp.dot(latents.T, backward, preferred_element_type=jnp.float32)
    latent_grad = jnp.dot(backward, decoder.T, preferred_element_type=jnp.float32) + sparsity
    preact_grad = (latent_grad * 2.0 * positive * live_mask[:, None]).astype(jnp.bfloat16)
    encoder_grad = jnp.dot(centred.T, preact_grad, preferred_element_type=jnp.float32)
    bias_grad = jnp.sum(preact_grad.astype(jnp.float32), axis=0)
    logit_grad = (-jnp.sum(errors * ungated, axis=1) * gating * (1.0 - gating)).astype(jnp.bfloat16)
    router_grad = jnp.dot(logit_grad, in_rows, preferred_element_type=jnp.float32)
    centre_part = -jnp.sum(errors, axis=0) - jnp.dot(
        encoder.astype(jnp.float32), bias_grad, precision=lax.Precision.HIGHEST
    )
    return (encoder_grad, bias_grad, decoder_grad, router_grad, centre_part)


def flipped(index, bits):
    result, place = index, 1
    while place <= bits:
        if bits & place:
            result = result + (1 - 2 * lax.rem(lax.div(index, place), 2)) * place
        place *= 2
    return result


def partner_of(offset, members):
    return (
        flipped(lax.axis_index("group"), offset // members),
        flipped(lax.axis_index("member"), offset % members),
    )


def greet(devices, members):
    barrier = pltpu.get_barrier_semaphore()
    for offset in range(1, devices):
        pl.semaphore_signal(
            barrier, inc=1, device_id=partner_of(offset, members), device_id_type=MESH
        )
    pl.semaphore_wait(barrier, devices - 1)


def dispatch_order(devices, members):
    half = members // 2
    near = [offset for offset in range(devices) if not offset & half]
    return near + [offset + half for offset in near]


def dispatch_kernel(
    devices,
    members,
    packed_ref,
    centre_ref,
    router_ref,
    encoder_ref,
    bias_ref,
    decoder_ref,
    rows_ref,
    outgoing_ref,
    positive_ref,
    ungated_ref,
    gating_ref,
    encoder_buf,
    decoder_buf,
    local_sem,
    send_sem,
    recv_sem,
):
    me = lax.axis_index("group") * members + lax.axis_index("member")
    slot_cap = packed_ref.shape[1]
    order = dispatch_order(devices, members)
    greet(devices, members)
    copies = [None] * devices
    half = devices // 2
    for step in range(devices):
        place = step // 2 if step % 2 else half + step // 2
        if order[place] == 0:
            continue
        group, member = partner_of(order[place], members)
        copies[place] = pltpu.make_async_remote_copy(
            src_ref=packed_ref.at[group * members + member],
            dst_ref=rows_ref.at[place],
            send_sem=send_sem.at[place],
            recv_sem=recv_sem.at[place],
            device_id=(group, member),
            device_id_type=MESH,
        )
        copies[place].start()
    own = pltpu.make_async_copy(packed_ref.at[me], rows_ref.at[0], local_sem.at[0])
    first = pltpu.make_async_copy(encoder_ref, encoder_buf, local_sem.at[1])
    second = pltpu.make_async_copy(decoder_ref, decoder_buf, local_sem.at[2])
    own.start()
    first.start()
    second.start()
    own.wait()
    first.wait()
    second.wait()
    per_chunk = max(1, 128 // slot_cap)
    centre = centre_ref[...]
    router = router_ref[...].astype(jnp.float32)
    for start in range(0, devices, per_chunk):
        places = range(start, min(start + per_chunk, devices))
        for place in places:
            if copies[place] is not None:
                copies[place].wait_recv()
        amount = len(places) * slot_cap
        chunk = pl.ds(start * slot_cap, amount)
        rows = rows_ref[pl.ds(start, len(places))].reshape(amount, rows_ref.shape[2])
        wide = rows.astype(jnp.float32)
        gating = jax.nn.sigmoid(jnp.sum(wide * router, axis=1, keepdims=True))
        centred = (wide - centre).astype(jnp.bfloat16)
        preact = (
            jnp.dot(centred, encoder_buf[...], preferred_element_type=jnp.float32) + bias_ref[...]
        )
        positive = jnp.maximum(preact, 0.0)
        latents = (positive * positive).astype(jnp.bfloat16)
        ungated = jnp.dot(latents, decoder_buf[...], preferred_element_type=jnp.float32)
        rebuilt = (centre + gating * ungated).astype(jnp.bfloat16)
        for number, place in enumerate(places):
            group, member = partner_of(order[place], members)
            outgoing_ref[group * members + member] = rebuilt[
                number * slot_cap : (number + 1) * slot_cap
            ]
        positive_ref[chunk] = positive
        ungated_ref[chunk] = ungated
        gating_ref[chunk] = jnp.broadcast_to(gating, (amount, gating_ref.shape[1]))
    for copy in copies:
        if copy is not None:
            copy.wait_send()


def dispatch_and_forward(packed, centre_bias, router_row, encoder, enc_bias, decoder, members):
    devices, slot_cap, features = packed.shape
    latent_count = encoder.shape[1]
    slots = devices * slot_cap
    in_vmem = pl.BlockSpec(memory_space=pltpu.VMEM)
    anywhere = pl.BlockSpec(memory_space=pl.ANY)
    return pl.pallas_call(
        functools.partial(dispatch_kernel, devices, members),
        out_shape=(
            jax.ShapeDtypeStruct((devices, slot_cap, features), jnp.bfloat16),
            jax.ShapeDtypeStruct((devices, slot_cap, features), jnp.bfloat16),
            jax.ShapeDtypeStruct((slots, latent_count), jnp.float32),
            jax.ShapeDtypeStruct((slots, features), jnp.float32),
            jax.ShapeDtypeStruct((slots, 128), jnp.float32),
        ),
        in_specs=[anywhere, in_vmem, in_vmem, anywhere, in_vmem, anywhere],
        out_specs=(in_vmem,) * 5,
        scratch_shapes=[
            pltpu.VMEM(encoder.shape, encoder.dtype),
            pltpu.VMEM(decoder.shape, decoder.dtype),
            pltpu.SemaphoreType.DMA((3,)),
            pltpu.SemaphoreType.DMA((devices,)),
            pltpu.SemaphoreType.DMA((devices,)),
        ],
        compiler_params=pltpu.CompilerParams(
            collective_id=0, has_side_effects=True, vmem_limit_bytes=32 << 20
        ),
        name="dispatch_forward",
    )(packed, centre_bias[None], router_row[None], encoder, enc_bias[None], decoder)


def centre_kernel(devices, members, part_ref, total_ref, parts, send_sem, recv_sem):
    greet(devices, members)
    copies = []
    for offset in range(1, devices):
        copies.append(
            pltpu.make_async_remote_copy(
                src_ref=part_ref,
                dst_ref=parts.at[lax.axis_index("group") * members + lax.axis_index("member")],
                send_sem=send_sem.at[offset],
                recv_sem=recv_sem.at[offset],
                device_id=partner_of(offset, members),
                device_id_type=MESH,
            )
        )
        copies[-1].start()
    parts[lax.axis_index("group") * members + lax.axis_index("member")] = part_ref[...]
    for copy in copies:
        copy.wait_recv()
    total_ref[...] = jnp.sum(parts[...], axis=0)
    for copy in copies:
        copy.wait_send()


def centre_sum(part, devices, members):
    shape = (1, part.shape[0])
    return pl.pallas_call(
        functools.partial(centre_kernel, devices, members),
        out_shape=jax.ShapeDtypeStruct(shape, jnp.float32),
        in_specs=[pl.BlockSpec(memory_space=pltpu.VMEM)],
        out_specs=pl.BlockSpec(memory_space=pltpu.VMEM),
        scratch_shapes=[
            pltpu.VMEM((devices,) + shape, jnp.float32),
            pltpu.SemaphoreType.DMA((devices,)),
            pltpu.SemaphoreType.DMA((devices,)),
        ],
        compiler_params=pltpu.CompilerParams(
            collective_id=1, has_side_effects=True, vmem_limit_bytes=4 << 20
        ),
        name="centre_sum",
    )(part[None])[0]


def power_of_two(number):
    return number & (number - 1) == 0


def per_device(
    activations,
    routes,
    centre_bias,
    centre_first,
    centre_second,
    router,
    router_first,
    router_second,
    encoder,
    enc_bias,
    decoder,
    encoder_first,
    encoder_second,
    enc_bias_first,
    enc_bias_second,
    decoder_first,
    decoder_second,
):
    groups = lax.axis_size("group")
    members = lax.axis_size("member")
    devices = groups * members
    row_count = activations.shape[0]
    feature_count = activations.shape[1]
    slot_cap = 2 * row_count // devices
    route_ids = routes[:, 0]
    onehot = (route_ids[:, None] == jnp.arange(devices, dtype=jnp.int32)[None, :]).astype(
        jnp.bfloat16
    )
    earlier = (jnp.arange(row_count)[:, None] > jnp.arange(row_count)[None, :]).astype(jnp.bfloat16)
    before = jnp.dot(earlier, onehot, preferred_element_type=jnp.float32)
    slot_rank = jnp.sum(before * onehot.astype(jnp.float32), axis=1).astype(jnp.int32)
    position = route_ids * slot_cap + slot_rank
    chosen = jnp.arange(devices * slot_cap, dtype=jnp.int32)[:, None] == position[None, :]
    select = chosen.astype(jnp.bfloat16)
    used = jnp.any(chosen, axis=1)
    packed = jnp.where(
        used[:, None],
        jnp.dot(select, activations, preferred_element_type=jnp.float32),
        EMPTY,
    ).astype(jnp.bfloat16)
    packed = packed.reshape(devices, slot_cap, feature_count)
    aligned = slot_cap % 16 == 0 and power_of_two(groups) and power_of_two(members)
    if aligned and members > 1:
        arrived, outgoing, positive, ungated, gating_wide = dispatch_and_forward(
            packed, centre_bias, router[0], encoder[0], enc_bias[0], decoder[0], members
        )
        in_rows = arrived.reshape(devices * slot_cap, feature_count)
        gating = gating_wide[:, 0]
        centred = (in_rows.astype(jnp.float32) - centre_bias).astype(jnp.bfloat16)
        latents = (positive * positive).astype(jnp.bfloat16)
        rebuilt = centre_bias + gating[:, None] * ungated
    else:
        arrived = lax.all_to_all(
            packed, ("group", "member"), split_axis=0, concat_axis=0, tiled=True
        )
        in_rows = arrived.reshape(devices * slot_cap, feature_count)
        centred, positive, latents, gating, ungated, rebuilt = forward_pass(
            in_rows, centre_bias, router[0], encoder[0], enc_bias[0], decoder[0]
        )
        outgoing = rebuilt.astype(jnp.bfloat16)
    live_mask = (in_rows[:, 0] < 0.5 * EMPTY).astype(jnp.float32)
    returned = lax.all_to_all(
        outgoing.reshape(devices, slot_cap, feature_count),
        ("group", "member"),
        split_axis=0,
        concat_axis=0,
        tiled=True,
    )
    recon = lax.dot_general(
        select,
        returned.reshape(devices * slot_cap, feature_count),
        (((0,), (0,)), ((), ())),
        preferred_element_type=jnp.float32,
    ).astype(jnp.bfloat16)
    encoder_grad, bias_grad, decoder_grad, router_grad, centre_part = backward_pass(
        in_rows,
        live_mask,
        centred,
        positive,
        latents,
        gating,
        ungated,
        rebuilt,
        encoder[0],
        decoder[0],
    )
    router_new = adam_update(router[0], router_grad, router_first[0], router_second[0])
    encoder_new = adam_update(encoder[0], encoder_grad, encoder_first[0], encoder_second[0])
    bias_new = adam_update(enc_bias[0], bias_grad, enc_bias_first[0], enc_bias_second[0])
    decoder_new = adam_update(decoder[0], decoder_grad, decoder_first[0], decoder_second[0])
    if power_of_two(groups) and power_of_two(members):
        centre_total = centre_sum(centre_part, devices, members)
    else:
        centre_total = lax.psum(centre_part, ("group", "member"))
    centre_new = adam_update(centre_bias, centre_total, centre_first, centre_second)
    return (
        recon,
        centre_new[0],
        centre_new[1],
        centre_new[2],
        router_new[0][None],
        router_new[1][None],
        router_new[2][None],
        encoder_new[0][None],
        bias_new[0][None],
        decoder_new[0][None],
        encoder_new[1][None],
        encoder_new[2][None],
        bias_new[1][None],
        bias_new[2][None],
        decoder_new[1][None],
        decoder_new[2][None],
    )


def solution(mesh):
    placed = (
        P(("group", "member"), None),
        P(("group", "member"), None),
        P(),
        P(),
        P(),
        P(("group", "member"), None),
        P(("group", "member"), None),
        P(("group", "member"), None),
        P(("group", "member"), None, None),
        P(("group", "member"), None),
        P(("group", "member"), None, None),
        P(("group", "member"), None, None),
        P(("group", "member"), None, None),
        P(("group", "member"), None),
        P(("group", "member"), None),
        P(("group", "member"), None, None),
        P(("group", "member"), None, None),
    )
    return jax.shard_map(
        per_device,
        mesh=mesh,
        in_specs=placed,
        out_specs=(
            P(("group", "member"), None),
            P(),
            P(),
            P(),
            P(("group", "member"), None),
            P(("group", "member"), None),
            P(("group", "member"), None),
            P(("group", "member"), None, None),
            P(("group", "member"), None),
            P(("group", "member"), None, None),
            P(("group", "member"), None, None),
            P(("group", "member"), None, None),
            P(("group", "member"), None),
            P(("group", "member"), None),
            P(("group", "member"), None, None),
            P(("group", "member"), None, None),
        ),
        check_vma=False,
    )
```

```python
import functools

import jax
import jax.numpy as jnp
from jax import lax
from jax.experimental import pallas as pl
from jax.experimental.pallas import tpu as pltpu
from jax.sharding import PartitionSpec as P

MESH = pl.DeviceIdType.MESH

STEP = 10


learn_rate = 0.001
beta_one = 0.9
beta_two = 0.999
adam_eps = 1e-08
sparsity = 0.1
EMPTY = 16.0


def adam_update(weights_in, gradient, moment_one, moment_two):
    first_new = beta_one * moment_one + (1.0 - beta_one) * gradient
    second_new = beta_two * moment_two + (1.0 - beta_two) * gradient * gradient
    first_hat = first_new / (1.0 - beta_one**STEP)
    second_hat = second_new / (1.0 - beta_two**STEP)
    stepped = weights_in.astype(jnp.float32) - learn_rate * first_hat / (
        jnp.sqrt(second_hat) + adam_eps
    )
    return (stepped.astype(weights_in.dtype), first_new, second_new)


def forward_pass(in_rows, centre_bias, router_row, encoder, enc_bias, decoder):
    centred = (in_rows.astype(jnp.float32) - centre_bias).astype(jnp.bfloat16)
    preact = jnp.dot(centred, encoder, preferred_element_type=jnp.float32) + enc_bias
    positive = jnp.maximum(preact, 0.0)
    latents = (positive * positive).astype(jnp.bfloat16)
    router_wide = jnp.broadcast_to(router_row[:, None], (router_row.shape[0], 128))
    logits = jnp.dot(in_rows, router_wide, preferred_element_type=jnp.float32)[:, 0]
    gating = jax.nn.sigmoid(logits)
    ungated = jnp.dot(latents, decoder, preferred_element_type=jnp.float32)
    rebuilt = centre_bias + gating[:, None] * ungated
    return (centred, positive, latents, gating, ungated, rebuilt)


def backward_pass(
    in_rows, live_mask, centred, positive, latents, gating, ungated, rebuilt, encoder, decoder
):
    errors = (in_rows.astype(jnp.float32) - rebuilt) * live_mask[:, None]
    backward = (-gating[:, None] * errors).astype(jnp.bfloat16)
    decoder_grad = jnp.dot(latents.T, backward, preferred_element_type=jnp.float32)
    latent_grad = jnp.dot(backward, decoder.T, preferred_element_type=jnp.float32) + sparsity
    preact_grad = (latent_grad * 2.0 * positive * live_mask[:, None]).astype(jnp.bfloat16)
    encoder_grad = jnp.dot(centred.T, preact_grad, preferred_element_type=jnp.float32)
    bias_grad = jnp.sum(preact_grad.astype(jnp.float32), axis=0)
    logit_grad = (-jnp.sum(errors * ungated, axis=1) * gating * (1.0 - gating)).astype(jnp.bfloat16)
    router_grad = jnp.dot(logit_grad, in_rows, preferred_element_type=jnp.float32)
    centre_part = -jnp.sum(errors, axis=0) - jnp.dot(
        encoder.astype(jnp.float32), bias_grad, precision=lax.Precision.HIGHEST
    )
    return (encoder_grad, bias_grad, decoder_grad, router_grad, centre_part)


def flipped(index, bits):
    result, place = index, 1
    while place <= bits:
        if bits & place:
            result = result + (1 - 2 * lax.rem(lax.div(index, place), 2)) * place
        place *= 2
    return result


def partner_of(offset, members):
    return (
        flipped(lax.axis_index("group"), offset // members),
        flipped(lax.axis_index("member"), offset % members),
    )


def greet(devices, members):
    barrier = pltpu.get_barrier_semaphore()
    for offset in range(1, devices):
        pl.semaphore_signal(
            barrier, inc=1, device_id=partner_of(offset, members), device_id_type=MESH
        )
    pl.semaphore_wait(barrier, devices - 1)


def dispatch_order(devices, members):
    half = members // 2
    near = [offset for offset in range(devices) if not offset & half]
    return near + [offset + half for offset in near]


def three_parts(values):
    high = values.astype(jnp.bfloat16).astype(jnp.float32)
    middle = (values - high).astype(jnp.bfloat16).astype(jnp.float32)
    low = values - high - middle
    row = lax.broadcasted_iota(jnp.int32, (16, values.shape[1]), 0)
    stacked = jnp.where(
        row == 0, high, jnp.where(row == 1, middle, jnp.where(row == 2, low, 0.0))
    )
    return stacked.astype(jnp.bfloat16)


def dispatch_kernel(
    devices,
    members,
    packed_ref,
    centre_ref,
    router_ref,
    encoder_ref,
    bias_ref,
    decoder_ref,
    outgoing_ref,
    centred_ref,
    latents_ref,
    backward_ref,
    preact_grad_ref,
    centre_part_ref,
    bias_grad_ref,
    router_grad_ref,
    encoder_buf,
    decoder_buf,
    rows_buf,
    outgoing_buf,
    centred_buf,
    latents_buf,
    backward_buf,
    preact_grad_buf,
    local_sem,
    out_sem,
    save_sem,
    send_sem,
    recv_sem,
):
    me = lax.axis_index("group") * members + lax.axis_index("member")
    slot_cap = packed_ref.shape[1]
    features = packed_ref.shape[2]
    order = dispatch_order(devices, members)
    greet(devices, members)
    copies = [None] * devices
    half = devices // 2
    for step in range(devices):
        place = step // 2 if step % 2 else half + step // 2
        if order[place] == 0:
            continue
        group, member = partner_of(order[place], members)
        copies[place] = pltpu.make_async_remote_copy(
            src_ref=packed_ref.at[group * members + member],
            dst_ref=rows_buf.at[place],
            send_sem=send_sem.at[place],
            recv_sem=recv_sem.at[place],
            device_id=(group, member),
            device_id_type=MESH,
        )
        copies[place].start()
    own = pltpu.make_async_copy(packed_ref.at[me], rows_buf.at[0], local_sem.at[0])
    first = pltpu.make_async_copy(encoder_ref, encoder_buf, local_sem.at[1])
    second = pltpu.make_async_copy(decoder_ref, decoder_buf, local_sem.at[2])
    own.start()
    first.start()
    second.start()
    own.wait()
    first.wait()
    second.wait()
    per_chunk = max(1, 128 // slot_cap)
    centre = centre_ref[...]
    router = router_ref[...].astype(jnp.float32)
    error_sum = jnp.zeros((1, features), jnp.float32)
    router_grad = jnp.zeros((1, features), jnp.float32)
    bias_grad = jnp.zeros(bias_ref.shape, jnp.float32)
    saves = []
    for start in range(0, devices, per_chunk):
        places = range(start, min(start + per_chunk, devices))
        for place in places:
            if copies[place] is not None:
                copies[place].wait_recv()
        amount = len(places) * slot_cap
        chunk = pl.ds(start * slot_cap, amount)
        wide = rows_buf[pl.ds(start, len(places))].reshape(amount, features).astype(jnp.float32)
        live = (wide[:, :1] < 0.5 * EMPTY).astype(jnp.float32)
        gating = jax.nn.sigmoid(jnp.sum(wide * router, axis=1, keepdims=True))
        centred = (wide - centre).astype(jnp.bfloat16)
        preact = (
            jnp.dot(centred, encoder_buf[...], preferred_element_type=jnp.float32) + bias_ref[...]
        )
        positive = jnp.maximum(preact, 0.0)
        latents = (positive * positive).astype(jnp.bfloat16)
        ungated = jnp.dot(latents, decoder_buf[...], preferred_element_type=jnp.float32)
        rebuilt = centre + gating * ungated
        outgoing_buf[pl.ds(start, len(places))] = rebuilt.astype(jnp.bfloat16).reshape(
            len(places), slot_cap, features
        )
        for place in places:
            group, member = partner_of(order[place], members)
            saves.append(
                pltpu.make_async_copy(
                    outgoing_buf.at[place],
                    outgoing_ref.at[group * members + member],
                    out_sem.at[place],
                )
            )
            saves[-1].start()
        errors = (wide - rebuilt) * live
        backward = (-gating * errors).astype(jnp.bfloat16)
        latent_grad = (
            lax.dot_general(
                backward,
                decoder_buf[...],
                (((1,), (1,)), ((), ())),
                preferred_element_type=jnp.float32,
            )
            + sparsity
        )
        preact_grad = (latent_grad * 2.0 * positive * live).astype(jnp.bfloat16)
        logit_grad = -jnp.sum(errors * ungated, axis=1, keepdims=True) * gating * (1.0 - gating)
        logit_grad = logit_grad.astype(jnp.bfloat16).astype(jnp.float32)
        error_sum = error_sum + jnp.sum(errors, axis=0, keepdims=True)
        router_grad = router_grad + jnp.sum(logit_grad * wide, axis=0, keepdims=True)
        bias_grad = bias_grad + jnp.sum(preact_grad.astype(jnp.float32), axis=0, keepdims=True)
        for number, (value, buf, ref) in enumerate(
            (
                (centred, centred_buf, centred_ref),
                (latents, latents_buf, latents_ref),
                (backward, backward_buf, backward_ref),
                (preact_grad, preact_grad_buf, preact_grad_ref),
            )
        ):
            buf[chunk] = value
            saves.append(
                pltpu.make_async_copy(
                    buf.at[chunk], ref.at[chunk], save_sem.at[start // per_chunk, number]
                )
            )
            saves[-1].start()
    bias_grad_ref[...] = bias_grad
    router_grad_ref[...] = router_grad
    products = lax.dot_general(
        three_parts(bias_grad),
        encoder_buf[...],
        (((1,), (1,)), ((), ())),
        preferred_element_type=jnp.float32,
    )
    centre_part_ref[...] = -error_sum - jnp.sum(products, axis=0, keepdims=True)
    for save in saves:
        save.wait()
    for copy in copies:
        if copy is not None:
            copy.wait_send()


def dispatch_and_compute(packed, centre_bias, router_row, encoder, enc_bias, decoder, members):
    devices, slot_cap, features = packed.shape
    latent_count = encoder.shape[1]
    slots = devices * slot_cap
    chunks = -(-devices // max(1, 128 // slot_cap))
    in_vmem = pl.BlockSpec(memory_space=pltpu.VMEM)
    anywhere = pl.BlockSpec(memory_space=pl.ANY)
    wide, narrow = (slots, features), (slots, latent_count)
    return pl.pallas_call(
        functools.partial(dispatch_kernel, devices, members),
        out_shape=(
            jax.ShapeDtypeStruct(packed.shape, jnp.bfloat16),
            jax.ShapeDtypeStruct(wide, jnp.bfloat16),
            jax.ShapeDtypeStruct(narrow, jnp.bfloat16),
            jax.ShapeDtypeStruct(wide, jnp.bfloat16),
            jax.ShapeDtypeStruct(narrow, jnp.bfloat16),
            jax.ShapeDtypeStruct((1, features), jnp.float32),
            jax.ShapeDtypeStruct((1, latent_count), jnp.float32),
            jax.ShapeDtypeStruct((1, features), jnp.float32),
        ),
        in_specs=[anywhere, in_vmem, in_vmem, anywhere, in_vmem, anywhere],
        out_specs=(anywhere,) * 5 + (in_vmem,) * 3,
        scratch_shapes=[
            pltpu.VMEM(encoder.shape, encoder.dtype),
            pltpu.VMEM(decoder.shape, decoder.dtype),
            pltpu.VMEM(packed.shape, jnp.bfloat16),
            pltpu.VMEM(packed.shape, jnp.bfloat16),
            pltpu.VMEM(wide, jnp.bfloat16),
            pltpu.VMEM(narrow, jnp.bfloat16),
            pltpu.VMEM(wide, jnp.bfloat16),
            pltpu.VMEM(narrow, jnp.bfloat16),
            pltpu.SemaphoreType.DMA((3,)),
            pltpu.SemaphoreType.DMA((devices,)),
            pltpu.SemaphoreType.DMA((chunks, 4)),
            pltpu.SemaphoreType.DMA((devices,)),
            pltpu.SemaphoreType.DMA((devices,)),
        ],
        compiler_params=pltpu.CompilerParams(
            collective_id=0, has_side_effects=True, vmem_limit_bytes=61 << 20
        ),
        name="dispatch_compute",
    )(packed, centre_bias[None], router_row[None], encoder, enc_bias[None], decoder)


def centre_kernel(devices, members, part_ref, total_ref, parts, send_sem, recv_sem):
    greet(devices, members)
    copies = []
    for offset in range(1, devices):
        copies.append(
            pltpu.make_async_remote_copy(
                src_ref=part_ref,
                dst_ref=parts.at[lax.axis_index("group") * members + lax.axis_index("member")],
                send_sem=send_sem.at[offset],
                recv_sem=recv_sem.at[offset],
                device_id=partner_of(offset, members),
                device_id_type=MESH,
            )
        )
        copies[-1].start()
    parts[lax.axis_index("group") * members + lax.axis_index("member")] = part_ref[...]
    for copy in copies:
        copy.wait_recv()
    total_ref[...] = jnp.sum(parts[...], axis=0)
    for copy in copies:
        copy.wait_send()


def centre_sum(part, devices, members):
    shape = (1, part.shape[0])
    return pl.pallas_call(
        functools.partial(centre_kernel, devices, members),
        out_shape=jax.ShapeDtypeStruct(shape, jnp.float32),
        in_specs=[pl.BlockSpec(memory_space=pltpu.VMEM)],
        out_specs=pl.BlockSpec(memory_space=pltpu.VMEM),
        scratch_shapes=[
            pltpu.VMEM((devices,) + shape, jnp.float32),
            pltpu.SemaphoreType.DMA((devices,)),
            pltpu.SemaphoreType.DMA((devices,)),
        ],
        compiler_params=pltpu.CompilerParams(
            collective_id=1, has_side_effects=True, vmem_limit_bytes=4 << 20
        ),
        name="centre_sum",
    )(part[None])[0]


def power_of_two(number):
    return number & (number - 1) == 0


def per_device(
    activations,
    routes,
    centre_bias,
    centre_first,
    centre_second,
    router,
    router_first,
    router_second,
    encoder,
    enc_bias,
    decoder,
    encoder_first,
    encoder_second,
    enc_bias_first,
    enc_bias_second,
    decoder_first,
    decoder_second,
):
    groups = lax.axis_size("group")
    members = lax.axis_size("member")
    devices = groups * members
    row_count = activations.shape[0]
    feature_count = activations.shape[1]
    slot_cap = 2 * row_count // devices
    route_ids = routes[:, 0]
    onehot = (route_ids[:, None] == jnp.arange(devices, dtype=jnp.int32)[None, :]).astype(
        jnp.bfloat16
    )
    earlier = (jnp.arange(row_count)[:, None] > jnp.arange(row_count)[None, :]).astype(jnp.bfloat16)
    before = jnp.dot(earlier, onehot, preferred_element_type=jnp.float32)
    slot_rank = jnp.sum(before * onehot.astype(jnp.float32), axis=1).astype(jnp.int32)
    position = route_ids * slot_cap + slot_rank
    chosen = jnp.arange(devices * slot_cap, dtype=jnp.int32)[:, None] == position[None, :]
    select = chosen.astype(jnp.bfloat16)
    used = jnp.any(chosen, axis=1)
    packed = jnp.where(
        used[:, None],
        jnp.dot(select, activations, preferred_element_type=jnp.float32),
        EMPTY,
    ).astype(jnp.bfloat16)
    packed = packed.reshape(devices, slot_cap, feature_count)
    aligned = slot_cap % 16 == 0 and power_of_two(groups) and power_of_two(members)
    aligned = aligned and members > 1
    if aligned:
        outgoing, centred, latents, backward, preact_grad, centre_part, bias_grad, router_grad = (
            dispatch_and_compute(
                packed, centre_bias, router[0], encoder[0], enc_bias[0], decoder[0], members
            )
        )
        centre_part, bias_grad, router_grad = centre_part[0], bias_grad[0], router_grad[0]
    else:
        arrived = lax.all_to_all(
            packed, ("group", "member"), split_axis=0, concat_axis=0, tiled=True
        )
        in_rows = arrived.reshape(devices * slot_cap, feature_count)
        live_mask = (in_rows[:, 0] < 0.5 * EMPTY).astype(jnp.float32)
        centred, positive, latents, gating, ungated, rebuilt = forward_pass(
            in_rows, centre_bias, router[0], encoder[0], enc_bias[0], decoder[0]
        )
        outgoing = rebuilt.astype(jnp.bfloat16)
    returned = lax.all_to_all(
        outgoing.reshape(devices, slot_cap, feature_count),
        ("group", "member"),
        split_axis=0,
        concat_axis=0,
        tiled=True,
    )
    recon = lax.dot_general(
        select,
        returned.reshape(devices * slot_cap, feature_count),
        (((0,), (0,)), ((), ())),
        preferred_element_type=jnp.float32,
    ).astype(jnp.bfloat16)
    if aligned:
        decoder_grad = jnp.dot(latents.T, backward, preferred_element_type=jnp.float32)
        encoder_grad = jnp.dot(centred.T, preact_grad, preferred_element_type=jnp.float32)
    else:
        encoder_grad, bias_grad, decoder_grad, router_grad, centre_part = backward_pass(
            in_rows,
            live_mask,
            centred,
            positive,
            latents,
            gating,
            ungated,
            rebuilt,
            encoder[0],
            decoder[0],
        )
    router_new = adam_update(router[0], router_grad, router_first[0], router_second[0])
    encoder_new = adam_update(encoder[0], encoder_grad, encoder_first[0], encoder_second[0])
    bias_new = adam_update(enc_bias[0], bias_grad, enc_bias_first[0], enc_bias_second[0])
    decoder_new = adam_update(decoder[0], decoder_grad, decoder_first[0], decoder_second[0])
    if power_of_two(groups) and power_of_two(members):
        centre_part, first, second = lax.optimization_barrier(
            (centre_part, encoder_new[1], decoder_new[1])
        )
        encoder_new = (encoder_new[0], first, encoder_new[2])
        decoder_new = (decoder_new[0], second, decoder_new[2])
        centre_total = centre_sum(centre_part, devices, members)
    else:
        centre_total = lax.psum(centre_part, ("group", "member"))
    centre_new = adam_update(centre_bias, centre_total, centre_first, centre_second)
    return (
        recon,
        centre_new[0],
        centre_new[1],
        centre_new[2],
        router_new[0][None],
        router_new[1][None],
        router_new[2][None],
        encoder_new[0][None],
        bias_new[0][None],
        decoder_new[0][None],
        encoder_new[1][None],
        encoder_new[2][None],
        bias_new[1][None],
        bias_new[2][None],
        decoder_new[1][None],
        decoder_new[2][None],
    )


def solution(mesh):
    placed = (
        P(("group", "member"), None),
        P(("group", "member"), None),
        P(),
        P(),
        P(),
        P(("group", "member"), None),
        P(("group", "member"), None),
        P(("group", "member"), None),
        P(("group", "member"), None, None),
        P(("group", "member"), None),
        P(("group", "member"), None, None),
        P(("group", "member"), None, None),
        P(("group", "member"), None, None),
        P(("group", "member"), None),
        P(("group", "member"), None),
        P(("group", "member"), None, None),
        P(("group", "member"), None, None),
    )
    return jax.shard_map(
        per_device,
        mesh=mesh,
        in_specs=placed,
        out_specs=(
            P(("group", "member"), None),
            P(),
            P(),
            P(),
            P(("group", "member"), None),
            P(("group", "member"), None),
            P(("group", "member"), None),
            P(("group", "member"), None, None),
            P(("group", "member"), None),
            P(("group", "member"), None, None),
            P(("group", "member"), None, None),
            P(("group", "member"), None, None),
            P(("group", "member"), None),
            P(("group", "member"), None),
            P(("group", "member"), None, None),
            P(("group", "member"), None, None),
        ),
        check_vma=False,
    )
```

```python
import functools

import jax
import jax.numpy as jnp
from jax import lax
from jax.experimental import pallas as pl
from jax.experimental.pallas import tpu as pltpu
from jax.sharding import PartitionSpec as P

MESH = pl.DeviceIdType.MESH

STEP = 10


learn_rate = 0.001
beta_one = 0.9
beta_two = 0.999
adam_eps = 1e-08
sparsity = 0.1
EMPTY = 16.0


def adam_update(weights_in, gradient, moment_one, moment_two):
    first_new = beta_one * moment_one + (1.0 - beta_one) * gradient
    second_new = beta_two * moment_two + (1.0 - beta_two) * gradient * gradient
    first_hat = first_new / (1.0 - beta_one**STEP)
    second_hat = second_new / (1.0 - beta_two**STEP)
    stepped = weights_in.astype(jnp.float32) - learn_rate * first_hat / (
        jnp.sqrt(second_hat) + adam_eps
    )
    return (stepped.astype(weights_in.dtype), first_new, second_new)


def forward_pass(in_rows, centre_bias, router_row, encoder, enc_bias, decoder):
    centred = (in_rows.astype(jnp.float32) - centre_bias).astype(jnp.bfloat16)
    preact = jnp.dot(centred, encoder, preferred_element_type=jnp.float32) + enc_bias
    positive = jnp.maximum(preact, 0.0)
    latents = (positive * positive).astype(jnp.bfloat16)
    router_wide = jnp.broadcast_to(router_row[:, None], (router_row.shape[0], 128))
    logits = jnp.dot(in_rows, router_wide, preferred_element_type=jnp.float32)[:, 0]
    gating = jax.nn.sigmoid(logits)
    ungated = jnp.dot(latents, decoder, preferred_element_type=jnp.float32)
    rebuilt = centre_bias + gating[:, None] * ungated
    return (centred, positive, latents, gating, ungated, rebuilt)


def backward_pass(
    in_rows, live_mask, centred, positive, latents, gating, ungated, rebuilt, encoder, decoder
):
    errors = (in_rows.astype(jnp.float32) - rebuilt) * live_mask[:, None]
    backward = (-gating[:, None] * errors).astype(jnp.bfloat16)
    decoder_grad = jnp.dot(latents.T, backward, preferred_element_type=jnp.float32)
    latent_grad = jnp.dot(backward, decoder.T, preferred_element_type=jnp.float32) + sparsity
    preact_grad = (latent_grad * 2.0 * positive * live_mask[:, None]).astype(jnp.bfloat16)
    encoder_grad = jnp.dot(centred.T, preact_grad, preferred_element_type=jnp.float32)
    bias_grad = jnp.sum(preact_grad.astype(jnp.float32), axis=0)
    logit_grad = (-jnp.sum(errors * ungated, axis=1) * gating * (1.0 - gating)).astype(jnp.bfloat16)
    router_grad = jnp.dot(logit_grad, in_rows, preferred_element_type=jnp.float32)
    centre_part = -jnp.sum(errors, axis=0) - jnp.dot(
        encoder.astype(jnp.float32), bias_grad, precision=lax.Precision.HIGHEST
    )
    return (encoder_grad, bias_grad, decoder_grad, router_grad, centre_part)


def flipped(index, bits):
    result, place = index, 1
    while place <= bits:
        if bits & place:
            result = result + (1 - 2 * lax.rem(lax.div(index, place), 2)) * place
        place *= 2
    return result


def partner_of(offset, members):
    return (
        flipped(lax.axis_index("group"), offset // members),
        flipped(lax.axis_index("member"), offset % members),
    )


def greet(devices, members):
    barrier = pltpu.get_barrier_semaphore()
    for offset in range(1, devices):
        pl.semaphore_signal(
            barrier, inc=1, device_id=partner_of(offset, members), device_id_type=MESH
        )
    pl.semaphore_wait(barrier, devices - 1)


def dispatch_order(devices, members):
    half = members // 2
    near = [offset for offset in range(devices) if not offset & half]
    return near + [offset + half for offset in near]


def three_parts(values):
    high = values.astype(jnp.bfloat16).astype(jnp.float32)
    middle = (values - high).astype(jnp.bfloat16).astype(jnp.float32)
    low = values - high - middle
    row = lax.broadcasted_iota(jnp.int32, (16, values.shape[1]), 0)
    stacked = jnp.where(
        row == 0, high, jnp.where(row == 1, middle, jnp.where(row == 2, low, 0.0))
    )
    return stacked.astype(jnp.bfloat16)


def dispatch_kernel(
    devices,
    members,
    packed_ref,
    centre_ref,
    router_ref,
    encoder_ref,
    bias_ref,
    decoder_ref,
    outgoing_ref,
    centred_ref,
    latents_ref,
    backward_ref,
    preact_grad_ref,
    centre_total_ref,
    bias_grad_ref,
    router_grad_ref,
    encoder_buf,
    decoder_buf,
    rows_buf,
    outgoing_buf,
    centred_buf,
    latents_buf,
    backward_buf,
    preact_grad_buf,
    local_sem,
    out_sem,
    save_sem,
    send_sem,
    recv_sem,
    part_buf,
    parts_buf,
    part_send_sem,
    part_recv_sem,
):
    me = lax.axis_index("group") * members + lax.axis_index("member")
    slot_cap = packed_ref.shape[1]
    features = packed_ref.shape[2]
    order = dispatch_order(devices, members)
    greet(devices, members)
    copies = [None] * devices
    half = devices // 2
    for step in range(devices):
        place = step // 2 if step % 2 else half + step // 2
        if order[place] == 0:
            continue
        group, member = partner_of(order[place], members)
        copies[place] = pltpu.make_async_remote_copy(
            src_ref=packed_ref.at[group * members + member],
            dst_ref=rows_buf.at[place],
            send_sem=send_sem.at[place],
            recv_sem=recv_sem.at[place],
            device_id=(group, member),
            device_id_type=MESH,
        )
        copies[place].start()
    own = pltpu.make_async_copy(packed_ref.at[me], rows_buf.at[0], local_sem.at[0])
    first = pltpu.make_async_copy(encoder_ref, encoder_buf, local_sem.at[1])
    second = pltpu.make_async_copy(decoder_ref, decoder_buf, local_sem.at[2])
    own.start()
    first.start()
    second.start()
    own.wait()
    first.wait()
    second.wait()
    per_chunk = max(1, 128 // slot_cap)
    centre = centre_ref[...]
    router = router_ref[...].astype(jnp.float32)
    error_sum = jnp.zeros((1, features), jnp.float32)
    router_grad = jnp.zeros((1, features), jnp.float32)
    bias_grad = jnp.zeros(bias_ref.shape, jnp.float32)
    saves = []
    for start in range(0, devices, per_chunk):
        places = range(start, min(start + per_chunk, devices))
        for place in places:
            if copies[place] is not None:
                copies[place].wait_recv()
        amount = len(places) * slot_cap
        chunk = pl.ds(start * slot_cap, amount)
        wide = rows_buf[pl.ds(start, len(places))].reshape(amount, features).astype(jnp.float32)
        live = (wide[:, :1] < 0.5 * EMPTY).astype(jnp.float32)
        gating = jax.nn.sigmoid(jnp.sum(wide * router, axis=1, keepdims=True))
        centred = (wide - centre).astype(jnp.bfloat16)
        preact = (
            jnp.dot(centred, encoder_buf[...], preferred_element_type=jnp.float32) + bias_ref[...]
        )
        positive = jnp.maximum(preact, 0.0)
        latents = (positive * positive).astype(jnp.bfloat16)
        ungated = jnp.dot(latents, decoder_buf[...], preferred_element_type=jnp.float32)
        rebuilt = centre + gating * ungated
        outgoing_buf[pl.ds(start, len(places))] = rebuilt.astype(jnp.bfloat16).reshape(
            len(places), slot_cap, features
        )
        for place in places:
            group, member = partner_of(order[place], members)
            saves.append(
                pltpu.make_async_copy(
                    outgoing_buf.at[place],
                    outgoing_ref.at[group * members + member],
                    out_sem.at[place],
                )
            )
            saves[-1].start()
        errors = (wide - rebuilt) * live
        backward = (-gating * errors).astype(jnp.bfloat16)
        latent_grad = (
            lax.dot_general(
                backward,
                decoder_buf[...],
                (((1,), (1,)), ((), ())),
                preferred_element_type=jnp.float32,
            )
            + sparsity
        )
        preact_grad = (latent_grad * 2.0 * positive * live).astype(jnp.bfloat16)
        logit_grad = -jnp.sum(errors * ungated, axis=1, keepdims=True) * gating * (1.0 - gating)
        logit_grad = logit_grad.astype(jnp.bfloat16).astype(jnp.float32)
        error_sum = error_sum + jnp.sum(errors, axis=0, keepdims=True)
        router_grad = router_grad + jnp.sum(logit_grad * wide, axis=0, keepdims=True)
        bias_grad = bias_grad + jnp.sum(preact_grad.astype(jnp.float32), axis=0, keepdims=True)
        for number, (value, buf, ref) in enumerate(
            (
                (centred, centred_buf, centred_ref),
                (latents, latents_buf, latents_ref),
                (backward, backward_buf, backward_ref),
                (preact_grad, preact_grad_buf, preact_grad_ref),
            )
        ):
            buf[chunk] = value
            saves.append(
                pltpu.make_async_copy(
                    buf.at[chunk], ref.at[chunk], save_sem.at[start // per_chunk, number]
                )
            )
            saves[-1].start()
    bias_grad_ref[...] = bias_grad
    router_grad_ref[...] = router_grad
    products = lax.dot_general(
        three_parts(bias_grad),
        encoder_buf[...],
        (((1,), (1,)), ((), ())),
        preferred_element_type=jnp.float32,
    )
    part = -error_sum - jnp.sum(products, axis=0, keepdims=True)
    part_buf[...] = part
    part_copies = []
    for offset in range(1, devices):
        part_copies.append(
            pltpu.make_async_remote_copy(
                src_ref=part_buf,
                dst_ref=parts_buf.at[me],
                send_sem=part_send_sem.at[offset],
                recv_sem=part_recv_sem.at[offset],
                device_id=partner_of(offset, members),
                device_id_type=MESH,
            )
        )
        part_copies[-1].start()
    parts_buf[me] = part
    for save in saves:
        save.wait()
    for copy in copies:
        if copy is not None:
            copy.wait_send()
    for copy in part_copies:
        copy.wait_recv()
    centre_total_ref[...] = jnp.sum(parts_buf[...], axis=0)
    for copy in part_copies:
        copy.wait_send()


def dispatch_and_compute(packed, centre_bias, router_row, encoder, enc_bias, decoder, members):
    devices, slot_cap, features = packed.shape
    latent_count = encoder.shape[1]
    slots = devices * slot_cap
    chunks = -(-devices // max(1, 128 // slot_cap))
    in_vmem = pl.BlockSpec(memory_space=pltpu.VMEM)
    anywhere = pl.BlockSpec(memory_space=pl.ANY)
    wide, narrow = (slots, features), (slots, latent_count)
    return pl.pallas_call(
        functools.partial(dispatch_kernel, devices, members),
        out_shape=(
            jax.ShapeDtypeStruct(packed.shape, jnp.bfloat16),
            jax.ShapeDtypeStruct(wide, jnp.bfloat16),
            jax.ShapeDtypeStruct(narrow, jnp.bfloat16),
            jax.ShapeDtypeStruct(wide, jnp.bfloat16),
            jax.ShapeDtypeStruct(narrow, jnp.bfloat16),
            jax.ShapeDtypeStruct((1, features), jnp.float32),
            jax.ShapeDtypeStruct((1, latent_count), jnp.float32),
            jax.ShapeDtypeStruct((1, features), jnp.float32),
        ),
        in_specs=[anywhere, in_vmem, in_vmem, anywhere, in_vmem, anywhere],
        out_specs=(anywhere,) * 5 + (in_vmem,) * 3,
        scratch_shapes=[
            pltpu.VMEM(encoder.shape, encoder.dtype),
            pltpu.VMEM(decoder.shape, decoder.dtype),
            pltpu.VMEM(packed.shape, jnp.bfloat16),
            pltpu.VMEM(packed.shape, jnp.bfloat16),
            pltpu.VMEM(wide, jnp.bfloat16),
            pltpu.VMEM(narrow, jnp.bfloat16),
            pltpu.VMEM(wide, jnp.bfloat16),
            pltpu.VMEM(narrow, jnp.bfloat16),
            pltpu.SemaphoreType.DMA((3,)),
            pltpu.SemaphoreType.DMA((devices,)),
            pltpu.SemaphoreType.DMA((chunks, 4)),
            pltpu.SemaphoreType.DMA((devices,)),
            pltpu.SemaphoreType.DMA((devices,)),
            pltpu.VMEM((1, features), jnp.float32),
            pltpu.VMEM((devices, 1, features), jnp.float32),
            pltpu.SemaphoreType.DMA((devices,)),
            pltpu.SemaphoreType.DMA((devices,)),
        ],
        compiler_params=pltpu.CompilerParams(
            collective_id=0, has_side_effects=True, vmem_limit_bytes=61 << 20
        ),
        name="dispatch_compute",
    )(packed, centre_bias[None], router_row[None], encoder, enc_bias[None], decoder)


def power_of_two(number):
    return number & (number - 1) == 0


def per_device(
    activations,
    routes,
    centre_bias,
    centre_first,
    centre_second,
    router,
    router_first,
    router_second,
    encoder,
    enc_bias,
    decoder,
    encoder_first,
    encoder_second,
    enc_bias_first,
    enc_bias_second,
    decoder_first,
    decoder_second,
):
    groups = lax.axis_size("group")
    members = lax.axis_size("member")
    devices = groups * members
    row_count = activations.shape[0]
    feature_count = activations.shape[1]
    slot_cap = 2 * row_count // devices
    route_ids = routes[:, 0]
    onehot = (route_ids[:, None] == jnp.arange(devices, dtype=jnp.int32)[None, :]).astype(
        jnp.bfloat16
    )
    earlier = (jnp.arange(row_count)[:, None] > jnp.arange(row_count)[None, :]).astype(jnp.bfloat16)
    before = jnp.dot(earlier, onehot, preferred_element_type=jnp.float32)
    slot_rank = jnp.sum(before * onehot.astype(jnp.float32), axis=1).astype(jnp.int32)
    position = route_ids * slot_cap + slot_rank
    chosen = jnp.arange(devices * slot_cap, dtype=jnp.int32)[:, None] == position[None, :]
    select = chosen.astype(jnp.bfloat16)
    used = jnp.any(chosen, axis=1)
    packed = jnp.where(
        used[:, None],
        jnp.dot(select, activations, preferred_element_type=jnp.float32),
        EMPTY,
    ).astype(jnp.bfloat16)
    packed = packed.reshape(devices, slot_cap, feature_count)
    aligned = slot_cap % 16 == 0 and power_of_two(groups) and power_of_two(members)
    aligned = aligned and members > 1
    if aligned:
        outgoing, centred, latents, backward, preact_grad, centre_total, bias_grad, router_grad = (
            dispatch_and_compute(
                packed, centre_bias, router[0], encoder[0], enc_bias[0], decoder[0], members
            )
        )
        centre_total, bias_grad, router_grad = centre_total[0], bias_grad[0], router_grad[0]
    else:
        arrived = lax.all_to_all(
            packed, ("group", "member"), split_axis=0, concat_axis=0, tiled=True
        )
        in_rows = arrived.reshape(devices * slot_cap, feature_count)
        live_mask = (in_rows[:, 0] < 0.5 * EMPTY).astype(jnp.float32)
        centred, positive, latents, gating, ungated, rebuilt = forward_pass(
            in_rows, centre_bias, router[0], encoder[0], enc_bias[0], decoder[0]
        )
        outgoing = rebuilt.astype(jnp.bfloat16)
    returned = lax.all_to_all(
        outgoing.reshape(devices, slot_cap, feature_count),
        ("group", "member"),
        split_axis=0,
        concat_axis=0,
        tiled=True,
    )
    recon = lax.dot_general(
        select,
        returned.reshape(devices * slot_cap, feature_count),
        (((0,), (0,)), ((), ())),
        preferred_element_type=jnp.float32,
    ).astype(jnp.bfloat16)
    if aligned:
        decoder_grad = jnp.dot(latents.T, backward, preferred_element_type=jnp.float32)
        encoder_grad = jnp.dot(centred.T, preact_grad, preferred_element_type=jnp.float32)
    else:
        encoder_grad, bias_grad, decoder_grad, router_grad, centre_part = backward_pass(
            in_rows,
            live_mask,
            centred,
            positive,
            latents,
            gating,
            ungated,
            rebuilt,
            encoder[0],
            decoder[0],
        )
    router_new = adam_update(router[0], router_grad, router_first[0], router_second[0])
    encoder_new = adam_update(encoder[0], encoder_grad, encoder_first[0], encoder_second[0])
    bias_new = adam_update(enc_bias[0], bias_grad, enc_bias_first[0], enc_bias_second[0])
    decoder_new = adam_update(decoder[0], decoder_grad, decoder_first[0], decoder_second[0])
    if not aligned:
        centre_total = lax.psum(centre_part, ("group", "member"))
    centre_new = adam_update(centre_bias, centre_total, centre_first, centre_second)
    return (
        recon,
        centre_new[0],
        centre_new[1],
        centre_new[2],
        router_new[0][None],
        router_new[1][None],
        router_new[2][None],
        encoder_new[0][None],
        bias_new[0][None],
        decoder_new[0][None],
        encoder_new[1][None],
        encoder_new[2][None],
        bias_new[1][None],
        bias_new[2][None],
        decoder_new[1][None],
        decoder_new[2][None],
    )


def solution(mesh):
    placed = (
        P(("group", "member"), None),
        P(("group", "member"), None),
        P(),
        P(),
        P(),
        P(("group", "member"), None),
        P(("group", "member"), None),
        P(("group", "member"), None),
        P(("group", "member"), None, None),
        P(("group", "member"), None),
        P(("group", "member"), None, None),
        P(("group", "member"), None, None),
        P(("group", "member"), None, None),
        P(("group", "member"), None),
        P(("group", "member"), None),
        P(("group", "member"), None, None),
        P(("group", "member"), None, None),
    )
    return jax.shard_map(
        per_device,
        mesh=mesh,
        in_specs=placed,
        out_specs=(
            P(("group", "member"), None),
            P(),
            P(),
            P(),
            P(("group", "member"), None),
            P(("group", "member"), None),
            P(("group", "member"), None),
            P(("group", "member"), None, None),
            P(("group", "member"), None),
            P(("group", "member"), None, None),
            P(("group", "member"), None, None),
            P(("group", "member"), None, None),
            P(("group", "member"), None),
            P(("group", "member"), None),
            P(("group", "member"), None, None),
            P(("group", "member"), None, None),
        ),
        check_vma=False,
    )
```
